32 devices in a mesh: tp: 4 (over z), sy: 4 (over x, core), sx: 2 (over y).
Axes of the slice: x: 2, y: 2, z: 4, core: 2. Of those that a mesh axis runs over, the one named last changes fastest.
Arguments:
- queries: bfloat16 [24, 4, 32, 16, 128], P('tp', None, 'sy', 'sx'), may hold values from -8 to 8
- key_vectors: bfloat16 [24, 4, 32, 16, 128], P('tp', None, 'sy', 'sx'), may hold values from -8 to 8
- value_vectors: bfloat16 [24, 4, 32, 16, 128], P('tp', None, 'sy', 'sx'), may hold values from -6 to 6
- out_grad: bfloat16 [24, 4, 32, 16, 128], P('tp', None, 'sy', 'sx'), may hold values from -6 to 6
- cell_valid: int32 [32, 16], replicated, may hold values from 0 to 1, as said below
Outputs:
- query_grad: bfloat16 [24, 4, 32, 16, 128], P('tp', None, 'sy', 'sx')
- key_grad: bfloat16 [24, 4, 32, 16, 128], P('tp', None, 'sy', 'sx')
- value_grad: bfloat16 [24, 4, 32, 16, 128], P('tp', None, 'sy', 'sx')
The draws below stay inside these ranges and needn't reach their ends.
Inputs may be any that keep to these rules, and one draw needn't show every extreme that they name: cell_valid is 1 exactly on one rectangle of cells and 0 elsewhere; the rectangle holds the rows 8 to 27 and the columns 4 to 11.
All inputs are finite; a program needn't handle non-finite values.
Results may differ from the reference program's by a relative error of at most 0.0085.
Values may be sent and summed in bfloat16 or wider, within the bound.
No kernel may reach another device: no remote copies, remote signals or barrier semaphores. Data moves between devices by JAX's collectives and lax.ppermute only.
A program may use at most 64 MiB of HBM per device.

```python
import math
import jax
import jax.numpy as jnp
from jax import lax

HEAD_COUNT = 24
HEAD_DIM = 128
FRAMES = 4
TILE_CELLS = 8
GRID_ROWS = 32
GRID_COLUMNS = 16


def draw_queries(key, part):
    sample = jax.random.normal(jax.random.fold_in(key, 1), (HEAD_COUNT, FRAMES, GRID_ROWS, GRID_COLUMNS, HEAD_DIM), jnp.float32)
    sample = jnp.clip(sample, -5.0, 5.0)
    return sample.astype(jnp.bfloat16)


def draw_key_vectors(key, part):
    sample = jax.random.normal(jax.random.fold_in(key, 2), (HEAD_COUNT, FRAMES, GRID_ROWS, GRID_COLUMNS, HEAD_DIM), jnp.float32)
    sample = jnp.clip(sample, -5.0, 5.0)
    return sample.astype(jnp.bfloat16)


def draw_cell_valid(key, part):
    subkeys = jax.random.split(jax.random.fold_in(key, 5), 4)
    upper_edge = jax.random.randint(subkeys[0], (), 0, GRID_ROWS // 4 + 1)
    lower_edge = GRID_ROWS - jax.random.randint(subkeys[1], (), 0, TILE_CELLS // 2 + 1)
    left_edge = jax.random.randint(subkeys[2], (), 0, GRID_COLUMNS // 4 + 1)
    right_edge = GRID_COLUMNS - jax.random.randint(subkeys[3], (), 0, TILE_CELLS // 2 + 1)
    row_number = jnp.arange(GRID_ROWS)
    column_number = jnp.arange(GRID_COLUMNS)
    row_inside = (row_number >= upper_edge) & (row_number < lower_edge)
    column_inside = (column_number >= left_edge) & (column_number < right_edge)
    return (row_inside[:, None] & column_inside[None, :]).astype(jnp.int32)


def steps_of(rng, dims, cuts, smallest, largest):
    loudness, own = 1.0, jax.random.fold_in(rng, 6)
    for dim, parts in cuts:
        draws = jnp.exp(jax.random.uniform(jax.random.fold_in(own, dim), (parts,), jnp.float32, smallest / len(cuts), largest / len(cuts)))
        loudness = loudness * jnp.repeat(draws, dims[dim] // parts).reshape([-1 if axis == dim else 1 for axis in range(len(dims))])
    return loudness


def normal_values(rng, dims, scale, limit, cuts=(), kind=jnp.bfloat16):
    values = scale * jax.random.normal(rng, dims, jnp.float32)
    if cuts:
        values = values * steps_of(rng, dims, cuts, -0.22, 0.18)
    return jnp.clip(values, -limit, limit).astype(kind)


def setup_inputs(seed: int = 0) -> dict:
    splits = jax.random.split(jax.random.key(seed), 6)
    queries = draw_queries(jax.random.fold_in(splits[5], 71), 0)
    key_vectors = draw_key_vectors(jax.random.fold_in(splits[5], 71), 0)
    value_vectors = normal_values(splits[2], (HEAD_COUNT, FRAMES, GRID_ROWS, GRID_COLUMNS, HEAD_DIM), 1.0, 6.0, ((0, 4), (2, 4), (3, 2)))
    out_grad = normal_values(splits[3], (HEAD_COUNT, FRAMES, GRID_ROWS, GRID_COLUMNS, HEAD_DIM), 1.0, 6.0, ((0, 4), (2, 4), (3, 2)))
    cell_valid = draw_cell_valid(jax.random.fold_in(splits[5], 71), 0)
    return dict(queries=queries, key_vectors=key_vectors, value_vectors=value_vectors, out_grad=out_grad, cell_valid=cell_valid)


def window_mask(cell_rim, frames, tile_size):
    rim_span = 3 * tile_size
    offset = jnp.arange(rim_span)[None, :] - tile_size - jnp.arange(tile_size)[:, None]
    inside = jnp.abs(offset) <= tile_size
    key_ok = cell_rim == 1
    query_ok = key_ok[tile_size:2 * tile_size, tile_size:2 * tile_size]
    cell_pairs = inside[:, None, :, None] & inside[None, :, None, :] & key_ok[None, None] & query_ok[:, :, None, None]
    allowed = jnp.broadcast_to(cell_pairs[None, :, :, None], (frames, tile_size, tile_size, frames, rim_span, rim_span))
    allowed = allowed.reshape(frames * tile_size * tile_size, frames * rim_span * rim_span)
    query_live = jnp.broadcast_to(query_ok[None], (frames, tile_size, tile_size)).reshape(-1)
    return (allowed, query_live)

def tile_pass(query_tile, grad_tile, key_rim, value_rim, allowed, query_live):
    width = query_tile.shape[-1]
    score_scale = 1.0 / math.sqrt(width)
    query_rows = query_tile.reshape(-1, width)
    grad_rows = grad_tile.reshape(-1, width)
    key_rows = key_rim.reshape(-1, width)
    value_rows = value_rim.reshape(-1, width)
    scores = jnp.dot(query_rows, key_rows.T, preferred_element_type=jnp.float32) * score_scale
    masked = jnp.where(allowed, scores, -jnp.inf)
    row_max = jnp.where(query_live, lax.optimization_barrier(jnp.max(masked, axis=1)), 0.0)
    unnormed = jnp.where(allowed, jnp.exp(scores - row_max[:, None]), 0.0)
    row_total = lax.optimization_barrier(jnp.sum(unnormed, axis=1)) + jnp.where(query_live, 0.0, 1.0)
    probs = unnormed / row_total[:, None]
    probs_low = probs.astype(jnp.bfloat16)
    attended = jnp.dot(probs_low, value_rows, preferred_element_type=jnp.float32)
    row_delta = lax.optimization_barrier(jnp.sum(grad_rows.astype(jnp.float32) * attended, axis=1))
    dprobs = jnp.dot(grad_rows, value_rows.T, preferred_element_type=jnp.float32)
    dscores = probs * (dprobs - row_delta[:, None])
    dscores_low = dscores.astype(jnp.bfloat16)
    query_part = jnp.dot(dscores_low, key_rows, preferred_element_type=jnp.float32) * score_scale
    key_part = (jnp.dot(dscores_low.T, query_rows, preferred_element_type=jnp.float32) * score_scale).astype(jnp.bfloat16)
    value_part = jnp.dot(probs_low.T, grad_rows, preferred_element_type=jnp.float32).astype(jnp.bfloat16)
    return (query_part.reshape(query_tile.shape), key_part.reshape(key_rim.shape), value_part.reshape(value_rim.shape))

def reference(queries, key_vectors, value_vectors, out_grad, cell_valid):
    rim_span = 3 * TILE_CELLS
    tile_columns = GRID_COLUMNS // TILE_CELLS
    tile_total = GRID_ROWS // TILE_CELLS * tile_columns
    valid_padded = jnp.pad(cell_valid, TILE_CELLS)
    spatial_pad = ((0, 0), (TILE_CELLS, TILE_CELLS), (TILE_CELLS, TILE_CELLS), (0, 0))

    def per_head(inputs):
        query_head, key_head, value_head, grad_head = inputs
        key_padded = jnp.pad(key_head, spatial_pad)
        value_padded = jnp.pad(value_head, spatial_pad)

        def step(running, tile_index):
            query_acc, side_acc = running
            row_start = (tile_index // tile_columns * TILE_CELLS).astype(jnp.int32)
            col_start = (tile_index % tile_columns * TILE_CELLS).astype(jnp.int32)
            zero_index = jnp.zeros((), jnp.int32)
            query_tile = lax.dynamic_slice(query_head, (zero_index, row_start, col_start, zero_index), (FRAMES, TILE_CELLS, TILE_CELLS, HEAD_DIM))
            grad_tile = lax.dynamic_slice(grad_head, (zero_index, row_start, col_start, zero_index), (FRAMES, TILE_CELLS, TILE_CELLS, HEAD_DIM))
            key_rim = lax.dynamic_slice(key_padded, (zero_index, row_start, col_start, zero_index), (FRAMES, rim_span, rim_span, HEAD_DIM))
            value_rim = lax.dynamic_slice(value_padded, (zero_index, row_start, col_start, zero_index), (FRAMES, rim_span, rim_span, HEAD_DIM))
            cell_rim = lax.dynamic_slice(valid_padded, (row_start, col_start), (rim_span, rim_span))
            allowed, query_live = window_mask(cell_rim, FRAMES, TILE_CELLS)
            query_part, key_part, value_part = tile_pass(query_tile, grad_tile, key_rim, value_rim, allowed, query_live)
            query_acc = lax.dynamic_update_slice(query_acc, query_part, (zero_index, row_start, col_start, zero_index))
            where_side = (zero_index, zero_index, row_start, col_start, zero_index)
            current = lax.dynamic_slice(side_acc, where_side, (2, FRAMES, rim_span, rim_span, HEAD_DIM))
            added = current + jnp.stack([key_part, value_part]).astype(jnp.float32)
            side_acc = lax.dynamic_update_slice(side_acc, added, where_side)
            return ((query_acc, side_acc), None)
        start_state = (jnp.zeros((FRAMES, GRID_ROWS, GRID_COLUMNS, HEAD_DIM), jnp.float32), jnp.zeros((2, FRAMES, GRID_ROWS + 2 * TILE_CELLS, GRID_COLUMNS + 2 * TILE_CELLS, HEAD_DIM), jnp.float32))
        final_state, unused = lax.scan(step, start_state, jnp.arange(tile_total, dtype=jnp.int32))
        query_acc, side_acc = final_state
        side_sum = side_acc[:, :, TILE_CELLS:TILE_CELLS + GRID_ROWS, TILE_CELLS:TILE_CELLS + GRID_COLUMNS]
        return (query_acc.astype(jnp.bfloat16), side_sum[0].astype(jnp.bfloat16), side_sum[1].astype(jnp.bfloat16))
    query_grad, key_grad, value_grad = lax.map(per_head, (queries, key_vectors, value_vectors, out_grad))
    return (query_grad, key_grad, value_grad)
```

```python
import functools
import math

import jax
import jax.numpy as jnp
from jax import lax
from jax.experimental import pallas as pl
from jax.experimental.pallas import tpu as pltpu
from jax.sharding import PartitionSpec as P

MASKED = -1e30
VMEM_SPEC = pl.BlockSpec(memory_space=pltpu.VMEM)


def extended(block, sides, width):
    for axis, dim in sides:
        count = lax.axis_size(axis)
        forward = [(i, i + 1) for i in range(count - 1)]
        backward = [(target, source) for source, target in forward]
        low = lax.ppermute(
            lax.slice_in_dim(block, block.shape[dim] - width, None, axis=dim), axis, forward
        )
        high = lax.ppermute(lax.slice_in_dim(block, 0, width, axis=dim), axis, backward)
        block = jnp.concatenate([low, block, high], axis=dim)
    return block


def passed_along(block, axis, distance):
    devices = range(lax.axis_size(axis))
    route = [(i - distance, i) for i in devices if i - distance in devices]
    return lax.ppermute(block, axis, route)


def window_mask(cell_rim, frames, tile_size):
    rim_span = 3 * tile_size
    offset = jnp.arange(rim_span)[None, :] - tile_size - jnp.arange(tile_size)[:, None]
    inside = jnp.abs(offset) <= tile_size
    key_ok = cell_rim == 1
    query_ok = key_ok[tile_size : 2 * tile_size, tile_size : 2 * tile_size]
    cell_pairs = (
        inside[:, None, :, None]
        & inside[None, :, None, :]
        & key_ok[None, None]
        & query_ok[:, :, None, None]
    )
    allowed = jnp.broadcast_to(
        cell_pairs[None, :, :, None], (frames, tile_size, tile_size, frames, rim_span, rim_span)
    )
    allowed = allowed.reshape(frames * tile_size * tile_size, frames * rim_span * rim_span)
    query_live = jnp.broadcast_to(query_ok[None], (frames, tile_size, tile_size)).reshape(-1)
    return (allowed, query_live)


def contract_last(left_rows, right_rows):
    return lax.dot_general(
        left_rows, right_rows, (((1,), (1,)), ((), ())), preferred_element_type=jnp.float32
    )


def contract_first(left_rows, right_rows):
    return lax.dot_general(
        left_rows, right_rows, (((0,), (0,)), ((), ())), preferred_element_type=jnp.float32
    )


def query_pass(query_rows, grad_rows, key_rows, value_rows, allowed, query_live, score_scale):
    scores = contract_last(query_rows, key_rows) * score_scale
    masked = jnp.where(allowed, scores, -jnp.inf)
    row_max = jnp.where(query_live, jnp.max(masked, axis=1), 0.0)
    unnormed = jnp.where(allowed, jnp.exp(scores - row_max[:, None]), 0.0)
    row_total = jnp.sum(unnormed, axis=1) + jnp.where(query_live, 0.0, 1.0)
    probs = unnormed / row_total[:, None]
    probs_low = probs.astype(jnp.bfloat16)
    attended = jnp.dot(probs_low, value_rows, preferred_element_type=jnp.float32)
    row_delta = jnp.sum(grad_rows.astype(jnp.float32) * attended, axis=1)
    dprobs = contract_last(grad_rows, value_rows)
    dscores_low = (probs * (dprobs - row_delta[:, None])).astype(jnp.bfloat16)
    query_part = jnp.dot(dscores_low, key_rows, preferred_element_type=jnp.float32) * score_scale
    return (probs_low, dscores_low, query_part, row_max, row_total, row_delta)


def general(queries, key_vectors, value_vectors, out_grad, cell_valid):
    tile_size = queries.shape[2]
    frames = queries.shape[1]
    width = queries.shape[-1]
    score_scale = 1.0 / math.sqrt(width)
    row_place = lax.axis_index("sy") * tile_size
    column_place = lax.axis_index("sx") * tile_size
    cell_rim = lax.dynamic_slice(
        jnp.pad(cell_valid, tile_size), (row_place, column_place), (3 * tile_size, 3 * tile_size)
    )
    allowed, query_live = window_mask(cell_rim, frames, tile_size)
    pair_local = jnp.stack([key_vectors, value_vectors], 1)
    pair_rims = extended(pair_local, (("sy", 3), ("sx", 4)), tile_size)

    def head_returned(inputs):
        query_head, grad_head, pair_rim = inputs
        query_rows = query_head.reshape(-1, width)
        grad_rows = grad_head.reshape(-1, width)
        probs_low, dscores_low, query_part, row_max, row_total, row_delta = query_pass(
            query_rows,
            grad_rows,
            pair_rim[0].reshape(-1, width),
            pair_rim[1].reshape(-1, width),
            allowed,
            query_live,
            score_scale,
        )
        key_part = (contract_first(dscores_low, query_rows) * score_scale).astype(jnp.bfloat16)
        value_part = contract_first(probs_low, grad_rows).astype(jnp.bfloat16)
        side_parts = jnp.stack([key_part, value_part]).reshape(pair_rim.shape)
        return (query_part.astype(jnp.bfloat16).reshape(query_head.shape), side_parts)

    query_grad, side_parts = lax.map(head_returned, (queries, out_grad, pair_rims))
    upper_band = side_parts[:, :, :, 0:tile_size]
    middle_rows = side_parts[:, :, :, tile_size : 2 * tile_size]
    lower_band = side_parts[:, :, :, 2 * tile_size : 3 * tile_size]
    below_parts = passed_along(upper_band, "sy", -1)
    above_parts = passed_along(lower_band, "sy", 1)
    row_sum = (
        middle_rows.astype(jnp.float32)
        + below_parts.astype(jnp.float32)
        + above_parts.astype(jnp.float32)
    )
    left_tile = row_sum[:, :, :, :, 0:tile_size]
    centre_tile = row_sum[:, :, :, :, tile_size : 2 * tile_size]
    right_tile = row_sum[:, :, :, :, 2 * tile_size : 3 * tile_size]
    right_parts = passed_along(left_tile, "sx", -1)
    left_parts = passed_along(right_tile, "sx", 1)
    side_total = centre_tile + right_parts + left_parts
    key_grad = side_total[:, 0].astype(jnp.bfloat16)
    value_grad = side_total[:, 1].astype(jnp.bfloat16)
    return (query_grad, key_grad, value_grad)


def pairs_of(count, first):
    low = range(first, count - 1, 2)
    return [(i, i + 1) for i in low] + [(i + 1, i) for i in low]


def bias_kernel(tile_size, place_ref, valid_ref, bias_ref):
    valid = valid_ref[...] == 1
    rows = lax.broadcasted_iota(jnp.int32, valid.shape, 0)
    columns = lax.broadcasted_iota(jnp.int32, valid.shape, 1)
    far = max(valid.shape)
    top = jnp.min(jnp.where(valid, rows, far))
    bottom = jnp.max(jnp.where(valid, rows, -1))
    left = jnp.min(jnp.where(valid, columns, far))
    right = jnp.max(jnp.where(valid, columns, -1))
    shape = bias_ref.shape[2:]
    key_cell = lax.broadcasted_iota(jnp.int32, shape, 0)
    query_cell = lax.broadcasted_iota(jnp.int32, shape, 1) % (tile_size * tile_size)
    key_row, key_column = key_cell // tile_size, key_cell % tile_size
    query_row, query_column = query_cell // tile_size, query_cell % tile_size

    def inside(row, column):
        return (row >= top) & (row <= bottom) & (column >= left) & (column <= right)

    for b in range(2):
        q_row = query_row + place_ref[0] * tile_size
        q_column = query_column + place_ref[3 + b] * tile_size
        q_ok = inside(q_row, q_column)
        for t in range(6):
            k_row = key_row + place_ref[t // 2] * tile_size
            k_column = key_column + place_ref[3 + t % 2] * tile_size
            near = (jnp.abs(k_row - q_row) <= tile_size) & (
                jnp.abs(k_column - q_column) <= tile_size
            )
            ok = near & q_ok & inside(k_row, k_column)
            bias_ref[b, t] = jnp.where(ok, 0.0, MASKED)


def window_bias(places, cell_valid, tile_size):
    cells = tile_size * tile_size
    return pl.pallas_call(
        functools.partial(bias_kernel, tile_size),
        out_shape=jax.ShapeDtypeStruct((2, 6, cells, 2 * cells), jnp.float32),
        in_specs=[pl.BlockSpec(memory_space=pltpu.SMEM), VMEM_SPEC],
        out_specs=VMEM_SPEC,
        name="window_bias",
    )(places, cell_valid)


def head_kernel(
    own_ref, partner_ref, even_ref, odd_ref, bias_ref,
    own_dq_ref, partner_dq_ref, middle_ref, even_part_ref, odd_part_ref,
    score_ref, dprob_ref, key_sum_ref, value_sum_ref,
):
    tokens, width = own_ref.shape[1:]
    score_scale = 1.0 / math.sqrt(width)
    exponent_scale = math.log2(math.e) / math.sqrt(width)
    keys = [own_ref.at[0], partner_ref.at[0], even_ref.at[0], even_ref.at[2], odd_ref.at[0], odd_ref.at[2]]
    values = [own_ref.at[1], partner_ref.at[1], even_ref.at[1], even_ref.at[3], odd_ref.at[1], odd_ref.at[3]]
    key_parts = [middle_ref.at[0], middle_ref.at[2], even_part_ref.at[0], even_part_ref.at[2], odd_part_ref.at[0], odd_part_ref.at[2]]
    value_parts = [middle_ref.at[1], middle_ref.at[3], even_part_ref.at[1], even_part_ref.at[3], odd_part_ref.at[1], odd_part_ref.at[3]]
    for b, (side, dq_ref) in enumerate(((own_ref, own_dq_ref), (partner_ref, partner_dq_ref))):
        query_rows = side[2]
        grad_rows = side[3]
        row_max = None
        for t in range(6):
            bias = bias_ref[b, t]
            bias = jnp.concatenate([bias] * (tokens // bias.shape[1]), axis=1)
            bias = jnp.concatenate([bias] * (tokens // bias.shape[0]), axis=0)
            scores = contract_last(keys[t][...], query_rows) + bias
            score_ref[t] = scores
            tile_max = jnp.max(scores, axis=0, keepdims=True)
            row_max = tile_max if row_max is None else jnp.maximum(row_max, tile_max)
        live = row_max > 0.5 * MASKED
        row_max = jnp.where(live, row_max, 0.0)
        row_total = jnp.where(live, 0.0, 1.0)
        row_delta = jnp.zeros_like(row_max)
        for t in range(6):
            unnormed = jnp.exp2((score_ref[t] - row_max) * exponent_scale)
            dprobs = contract_last(values[t][...], grad_rows)
            score_ref[t] = unnormed
            dprob_ref[t] = dprobs
            row_total = row_total + jnp.sum(unnormed, axis=0, keepdims=True)
            row_delta = row_delta + jnp.sum(unnormed * dprobs, axis=0, keepdims=True)
        inverse = 1.0 / row_total
        row_delta = row_delta * inverse
        query_grad = None
        for t in range(6):
            probs = score_ref[t] * inverse
            dscores_low = (probs * (dprob_ref[t] - row_delta)).astype(jnp.bfloat16)
            value_part = jnp.dot(
                probs.astype(jnp.bfloat16), grad_rows, preferred_element_type=jnp.float32
            )
            key_part = jnp.dot(dscores_low, query_rows, preferred_element_type=jnp.float32)
            if b == 0:
                key_sum_ref[t] = key_part
                value_sum_ref[t] = value_part
            else:
                key_total = (key_sum_ref[t] + key_part) * score_scale
                key_parts[t][...] = key_total.astype(middle_ref.dtype if t < 2 else jnp.bfloat16)
                value_total = value_sum_ref[t] + value_part
                value_parts[t][...] = value_total.astype(middle_ref.dtype if t < 2 else jnp.bfloat16)
            query_part = contract_first(dscores_low, keys[t][...])
            query_grad = query_part if query_grad is None else query_grad + query_part
        dq_ref[...] = (query_grad * score_scale).astype(jnp.bfloat16)


def head_grads(own, partner, even, odd, bias):
    tokens, width = own.shape[1:]
    low = jnp.bfloat16
    pairs = 2 * 6 * tokens * tokens
    return pl.pallas_call(
        head_kernel,
        out_shape=(
            jax.ShapeDtypeStruct((tokens, width), low),
            jax.ShapeDtypeStruct((tokens, width), low),
            jax.ShapeDtypeStruct((4, tokens, width), jnp.float32),
            jax.ShapeDtypeStruct((4, tokens, width), low),
            jax.ShapeDtypeStruct((4, tokens, width), low),
        ),
        in_specs=[VMEM_SPEC] * 5,
        out_specs=[VMEM_SPEC] * 5,
        scratch_shapes=[
            pltpu.VMEM((6, tokens, tokens), jnp.float32),
            pltpu.VMEM((6, tokens, tokens), jnp.float32),
            pltpu.VMEM((6, tokens, width), jnp.float32),
            pltpu.VMEM((6, tokens, width), jnp.float32),
        ],
        cost_estimate=pl.CostEstimate(
            flops=10 * pairs * width, transcendentals=pairs, bytes_accessed=20 * tokens * width * 2
        ),
        name="head_grads",
    )(own, partner, even, odd, bias)


def swapped(queries, key_vectors, value_vectors, out_grad, cell_valid):
    heads, frames, tile_size, _, width = queries.shape
    tokens = frames * tile_size * tile_size
    half = heads // 2
    rows = lax.axis_size("sy")
    row, column = lax.axis_index("sy"), lax.axis_index("sx")
    swap = [(0, 1), (1, 0)]
    even_pairs, odd_pairs = pairs_of(rows, 0), pairs_of(rows, 1)
    arrays = [a.reshape(heads, tokens, width) for a in (key_vectors, value_vectors, queries, out_grad)]

    def one_head(index):
        return jnp.concatenate(
            [lax.dynamic_slice_in_dim(a, index, 1, axis=0) for a in arrays], axis=0
        )

    even_row = row + 1 - 2 * (row % 2)
    odd_row = row - 1 + 2 * (row % 2)
    places = jnp.stack([row, even_row, odd_row, column, 1 - column]).astype(jnp.int32)
    received = [lax.ppermute(one_head((1 - column) * half + h), "sx", swap) for h in range(half)]
    bias = window_bias(places, cell_valid, tile_size)
    local_grads, returned = [], []
    for h in range(half):
        own = one_head(column * half + h)
        halo = jnp.concatenate([own[:2], received[h][:2]], axis=0)
        even = lax.ppermute(halo, "sy", even_pairs)
        odd = lax.ppermute(halo, "sy", odd_pairs)
        own_dq, partner_dq, middle, even_part, odd_part = head_grads(
            own, received[h], even, odd, bias
        )
        even_back = lax.ppermute(even_part, "sy", even_pairs)
        odd_back = lax.ppermute(odd_part, "sy", odd_pairs)
        total = middle + even_back.astype(jnp.float32) + odd_back.astype(jnp.float32)
        total = total.astype(jnp.bfloat16)
        local_grads.append(jnp.concatenate([own_dq[None], total[:2]], axis=0))
        outgoing = jnp.concatenate([partner_dq[None], total[2:]], axis=0)
        returned.append(lax.ppermute(outgoing, "sx", swap))
    first = column == 0
    outs = []
    for i in range(3):
        mine = jnp.stack([g[i] for g in local_grads])
        theirs = jnp.stack([g[i] for g in returned])
        out = jnp.concatenate(
            [jnp.where(first, mine, theirs), jnp.where(first, theirs, mine)], axis=0
        )
        outs.append(out.reshape(queries.shape))
    return tuple(outs)


def local(queries, *rest):
    if lax.axis_size("sx") == 2 and queries.shape[0] % 2 == 0:
        return swapped(queries, *rest)
    return general(queries, *rest)


def solution(mesh):
    return jax.shard_map(
        local,
        mesh=mesh,
        in_specs=(
            P("tp", None, "sy", "sx", None),
            P("tp", None, "sy", "sx", None),
            P("tp", None, "sy", "sx", None),
            P("tp", None, "sy", "sx", None),
            P(),
        ),
        out_specs=(
            P("tp", None, "sy", "sx", None),
            P("tp", None, "sy", "sx", None),
            P("tp", None, "sy", "sx", None),
        ),
        check_vma=False,
    )
```

```python
import functools
import math

import jax
import jax.numpy as jnp
from jax import lax
from jax.experimental import pallas as pl
from jax.experimental.pallas import tpu as pltpu
from jax.sharding import PartitionSpec as P

MASKED = -1e30
VMEM_SPEC = pl.BlockSpec(memory_space=pltpu.VMEM)
SMALL_GRANT = pltpu.CompilerParams(vmem_limit_bytes=16 * 2**20)


def on_chip(*arrays):
    return [pltpu.with_memory_space_constraint(a, pltpu.VMEM) for a in arrays]


def extended(block, sides, width):
    for axis, dim in sides:
        count = lax.axis_size(axis)
        forward = [(i, i + 1) for i in range(count - 1)]
        backward = [(target, source) for source, target in forward]
        low = lax.ppermute(
            lax.slice_in_dim(block, block.shape[dim] - width, None, axis=dim), axis, forward
        )
        high = lax.ppermute(lax.slice_in_dim(block, 0, width, axis=dim), axis, backward)
        block = jnp.concatenate([low, block, high], axis=dim)
    return block


def passed_along(block, axis, distance):
    devices = range(lax.axis_size(axis))
    route = [(i - distance, i) for i in devices if i - distance in devices]
    return lax.ppermute(block, axis, route)


def window_mask(cell_rim, frames, tile_size):
    rim_span = 3 * tile_size
    offset = jnp.arange(rim_span)[None, :] - tile_size - jnp.arange(tile_size)[:, None]
    inside = jnp.abs(offset) <= tile_size
    key_ok = cell_rim == 1
    query_ok = key_ok[tile_size : 2 * tile_size, tile_size : 2 * tile_size]
    cell_pairs = (
        inside[:, None, :, None]
        & inside[None, :, None, :]
        & key_ok[None, None]
        & query_ok[:, :, None, None]
    )
    allowed = jnp.broadcast_to(
        cell_pairs[None, :, :, None], (frames, tile_size, tile_size, frames, rim_span, rim_span)
    )
    allowed = allowed.reshape(frames * tile_size * tile_size, frames * rim_span * rim_span)
    query_live = jnp.broadcast_to(query_ok[None], (frames, tile_size, tile_size)).reshape(-1)
    return (allowed, query_live)


def contract_last(left_rows, right_rows):
    return lax.dot_general(
        left_rows, right_rows, (((1,), (1,)), ((), ())), preferred_element_type=jnp.float32
    )


def contract_first(left_rows, right_rows):
    return lax.dot_general(
        left_rows, right_rows, (((0,), (0,)), ((), ())), preferred_element_type=jnp.float32
    )


def query_pass(query_rows, grad_rows, key_rows, value_rows, allowed, query_live, score_scale):
    scores = contract_last(query_rows, key_rows) * score_scale
    masked = jnp.where(allowed, scores, -jnp.inf)
    row_max = jnp.where(query_live, jnp.max(masked, axis=1), 0.0)
    unnormed = jnp.where(allowed, jnp.exp(scores - row_max[:, None]), 0.0)
    row_total = jnp.sum(unnormed, axis=1) + jnp.where(query_live, 0.0, 1.0)
    probs = unnormed / row_total[:, None]
    probs_low = probs.astype(jnp.bfloat16)
    attended = jnp.dot(probs_low, value_rows, preferred_element_type=jnp.float32)
    row_delta = jnp.sum(grad_rows.astype(jnp.float32) * attended, axis=1)
    dprobs = contract_last(grad_rows, value_rows)
    dscores_low = (probs * (dprobs - row_delta[:, None])).astype(jnp.bfloat16)
    query_part = jnp.dot(dscores_low, key_rows, preferred_element_type=jnp.float32) * score_scale
    return (probs_low, dscores_low, query_part, row_max, row_total, row_delta)


def general(queries, key_vectors, value_vectors, out_grad, cell_valid):
    tile_size = queries.shape[2]
    frames = queries.shape[1]
    width = queries.shape[-1]
    score_scale = 1.0 / math.sqrt(width)
    row_place = lax.axis_index("sy") * tile_size
    column_place = lax.axis_index("sx") * tile_size
    cell_rim = lax.dynamic_slice(
        jnp.pad(cell_valid, tile_size), (row_place, column_place), (3 * tile_size, 3 * tile_size)
    )
    allowed, query_live = window_mask(cell_rim, frames, tile_size)
    pair_local = jnp.stack([key_vectors, value_vectors], 1)
    pair_rims = extended(pair_local, (("sy", 3), ("sx", 4)), tile_size)

    def head_returned(inputs):
        query_head, grad_head, pair_rim = inputs
        query_rows = query_head.reshape(-1, width)
        grad_rows = grad_head.reshape(-1, width)
        probs_low, dscores_low, query_part, _, _, _ = query_pass(
            query_rows,
            grad_rows,
            pair_rim[0].reshape(-1, width),
            pair_rim[1].reshape(-1, width),
            allowed,
            query_live,
            score_scale,
        )
        key_part = (contract_first(dscores_low, query_rows) * score_scale).astype(jnp.bfloat16)
        value_part = contract_first(probs_low, grad_rows).astype(jnp.bfloat16)
        side_parts = jnp.stack([key_part, value_part]).reshape(pair_rim.shape)
        return (query_part.astype(jnp.bfloat16).reshape(query_head.shape), side_parts)

    query_grad, side_parts = lax.map(head_returned, (queries, out_grad, pair_rims))
    upper_band = side_parts[:, :, :, 0:tile_size]
    middle_rows = side_parts[:, :, :, tile_size : 2 * tile_size]
    lower_band = side_parts[:, :, :, 2 * tile_size : 3 * tile_size]
    below_parts = passed_along(upper_band, "sy", -1)
    above_parts = passed_along(lower_band, "sy", 1)
    row_sum = (
        middle_rows.astype(jnp.float32)
        + below_parts.astype(jnp.float32)
        + above_parts.astype(jnp.float32)
    )
    left_tile = row_sum[:, :, :, :, 0:tile_size]
    centre_tile = row_sum[:, :, :, :, tile_size : 2 * tile_size]
    right_tile = row_sum[:, :, :, :, 2 * tile_size : 3 * tile_size]
    right_parts = passed_along(left_tile, "sx", -1)
    left_parts = passed_along(right_tile, "sx", 1)
    side_total = centre_tile + right_parts + left_parts
    key_grad = side_total[:, 0].astype(jnp.bfloat16)
    value_grad = side_total[:, 1].astype(jnp.bfloat16)
    return (query_grad, key_grad, value_grad)


def pairs_of(count, first):
    low = range(first, count - 1, 2)
    return [(i, i + 1) for i in low] + [(i + 1, i) for i in low]


def neighbour_rows(row):
    return row + 1 - 2 * lax.rem(row, 2), row - 1 + 2 * lax.rem(row, 2)


def copy_all(copies):
    for copy in copies:
        copy.start()
    for copy in copies:
        copy.wait()


def pack_kernel(picks, *refs):
    arrays, outs, sems = refs[:4], refs[4:-1], refs[-1]
    half = arrays[0].shape[0] // 2
    column = lax.axis_index("sx")
    copies = []
    for out, rows in zip(outs, picks):
        for slot, (array, h, mine) in enumerate(rows):
            head = (column if mine else 1 - column) * half + h
            copies.append(
                pltpu.make_async_copy(
                    arrays[array].at[head], out.at[slot], sems.at[len(copies)]
                )
            )
    copy_all(copies)


def packed(arrays, picks):
    tokens, width = arrays[0].shape[1:]
    return pl.pallas_call(
        functools.partial(pack_kernel, picks),
        out_shape=tuple(pltpu.VMEM((len(rows), tokens, width), jnp.bfloat16) for rows in picks),
        in_specs=[pl.BlockSpec(memory_space=pltpu.HBM)] * 4,
        out_specs=tuple(VMEM_SPEC for _ in picks),
        scratch_shapes=[pltpu.SemaphoreType.DMA((sum(map(len, picks)),))],
        compiler_params=SMALL_GRANT,
    )(*[pltpu.with_memory_space_constraint(a, pltpu.HBM) for a in arrays])


def bias_kernel(tile_size, valid_ref, bias_ref):
    row, column = lax.axis_index("sy"), lax.axis_index("sx")
    tile_rows = (row, *neighbour_rows(row))
    tile_columns = (column, 1 - column)
    valid = valid_ref[...] == 1
    rows = lax.broadcasted_iota(jnp.int32, valid.shape, 0)
    columns = lax.broadcasted_iota(jnp.int32, valid.shape, 1)
    far = max(valid.shape)
    top = jnp.min(jnp.where(valid, rows, far))
    bottom = jnp.max(jnp.where(valid, rows, -1))
    left = jnp.min(jnp.where(valid, columns, far))
    right = jnp.max(jnp.where(valid, columns, -1))
    shape = bias_ref.shape[2:]
    key_cell = lax.broadcasted_iota(jnp.int32, shape, 0)
    query_cell = lax.broadcasted_iota(jnp.int32, shape, 1) % (tile_size * tile_size)
    key_row, key_column = key_cell // tile_size, key_cell % tile_size
    query_row, query_column = query_cell // tile_size, query_cell % tile_size

    def inside(r, c):
        return (r >= top) & (r <= bottom) & (c >= left) & (c <= right)

    for b in range(2):
        q_row = query_row + row * tile_size
        q_column = query_column + tile_columns[b] * tile_size
        q_ok = inside(q_row, q_column)
        for t in range(6):
            k_row = key_row + tile_rows[t // 2] * tile_size
            k_column = key_column + tile_columns[t % 2] * tile_size
            near = (jnp.abs(k_row - q_row) <= tile_size) & (
                jnp.abs(k_column - q_column) <= tile_size
            )
            ok = near & q_ok & inside(k_row, k_column)
            bias_ref[b, t] = jnp.where(ok, 0.0, MASKED)


def window_bias(cell_valid, tile_size):
    cells = tile_size * tile_size
    return pl.pallas_call(
        functools.partial(bias_kernel, tile_size),
        out_shape=pltpu.VMEM((2, 6, cells, 2 * cells), jnp.float32),
        in_specs=[VMEM_SPEC],
        out_specs=VMEM_SPEC,
        compiler_params=SMALL_GRANT,
        name="window_bias",
    )(cell_valid)


def head_kernel(
    h, place,
    own_kv_ref, own_qg_ref, kv_ref, qg_ref, even_own_ref, even_ref, odd_own_ref, odd_ref, bias_ref,
    own_dq_ref, partner_dq_ref, middle_ref, even_part_ref, odd_part_ref,
    score_ref, dprob_ref, key_sum_ref, value_sum_ref,
):
    tokens, width = own_kv_ref.shape[1:]
    score_scale = 1.0 / math.sqrt(width)
    exponent_scale = math.log2(math.e) / math.sqrt(width)
    sides = ((own_kv_ref, kv_ref), (even_own_ref, even_ref), (odd_own_ref, odd_ref))
    keys, values = [
        [ref.at[first + i] for side in sides for ref, first in zip(side, (2 * h, place))]
        for i in range(2)
    ]
    key_parts, value_parts = [
        [part.at[2 * c + i] for part in (middle_ref, even_part_ref, odd_part_ref) for c in range(2)]
        for i in range(2)
    ]
    blocks = (
        (own_qg_ref[2 * h], own_qg_ref[2 * h + 1], own_dq_ref),
        (qg_ref[place], qg_ref[place + 1], partner_dq_ref),
    )
    for b, (query_rows, grad_rows, dq_ref) in enumerate(blocks):
        row_max = None
        for t in range(6):
            bias = bias_ref[b, t]
            bias = jnp.concatenate([bias] * (tokens // bias.shape[1]), axis=1)
            bias = jnp.concatenate([bias] * (tokens // bias.shape[0]), axis=0)
            scores = contract_last(keys[t][...], query_rows) + bias
            score_ref[t] = scores
            tile_max = jnp.max(scores, axis=0, keepdims=True)
            row_max = tile_max if row_max is None else jnp.maximum(row_max, tile_max)
        live = row_max > 0.5 * MASKED
        row_max = jnp.where(live, row_max, 0.0)
        row_total = jnp.where(live, 0.0, 1.0)
        row_delta = jnp.zeros_like(row_max)
        for t in range(6):
            unnormed = jnp.exp2((score_ref[t] - row_max) * exponent_scale)
            dprobs = contract_last(values[t][...], grad_rows)
            score_ref[t] = unnormed
            dprob_ref[t] = dprobs
            row_total = row_total + jnp.sum(unnormed, axis=0, keepdims=True)
            row_delta = row_delta + jnp.sum(unnormed * dprobs, axis=0, keepdims=True)
        inverse = 1.0 / row_total
        row_delta = row_delta * inverse
        query_grad = None
        for t in range(6):
            probs = score_ref[t] * inverse
            dscores_low = (probs * (dprob_ref[t] - row_delta)).astype(jnp.bfloat16)
            value_part = jnp.dot(
                probs.astype(jnp.bfloat16), grad_rows, preferred_element_type=jnp.float32
            )
            key_part = jnp.dot(dscores_low, query_rows, preferred_element_type=jnp.float32)
            if b == 0:
                key_sum_ref[t] = key_part
                value_sum_ref[t] = value_part
            else:
                key_total = (key_sum_ref[t] + key_part) * score_scale
                key_parts[t][...] = key_total.astype(key_parts[t].dtype)
                value_total = value_sum_ref[t] + value_part
                value_parts[t][...] = value_total.astype(value_parts[t].dtype)
            query_part = contract_first(dscores_low, keys[t][...])
            query_grad = query_part if query_grad is None else query_grad + query_part
        dq_ref[...] = (query_grad * score_scale).astype(jnp.bfloat16)


def head_grads(h, place, arrays, bias):
    tokens, width = arrays[0].shape[1:]
    low = jnp.bfloat16
    pairs = 2 * 6 * tokens * tokens
    return pl.pallas_call(
        functools.partial(head_kernel, h, place),
        out_shape=(
            pltpu.VMEM((tokens, width), low),
            pltpu.VMEM((tokens, width), low),
            pltpu.VMEM((4, tokens, width), jnp.float32),
            pltpu.VMEM((4, tokens, width), low),
            pltpu.VMEM((4, tokens, width), low),
        ),
        in_specs=[VMEM_SPEC] * 9,
        out_specs=[VMEM_SPEC] * 5,
        scratch_shapes=[
            pltpu.VMEM((6, tokens, tokens), jnp.float32),
            pltpu.VMEM((6, tokens, tokens), jnp.float32),
            pltpu.VMEM((6, tokens, width), jnp.float32),
            pltpu.VMEM((6, tokens, width), jnp.float32),
        ],
        compiler_params=SMALL_GRANT,
        cost_estimate=pl.CostEstimate(
            flops=10 * pairs * width, transcendentals=pairs, bytes_accessed=20 * tokens * width * 2
        ),
        name="head_grads",
    )(*on_chip(*arrays, bias))


def query_slots(half):
    return [(0, 2)] + [(h - 1, 2 + (h == 1)) for h in range(1, half)]


def collect_kernel(count, *refs):
    mine, theirs, outs, sems = refs[:count], refs[count:-4], refs[-4:-1], refs[-1]
    half = outs[0].shape[0] // 2
    column = lax.axis_index("sx")
    copies = []

    def send(source, out, head):
        copies.append(pltpu.make_async_copy(source, out.at[head], sems.at[len(copies)]))

    for h, (ref, slot) in enumerate(query_slots(half)):
        send(mine[2 * h], outs[0], column * half + h)
        send(theirs[ref].at[slot], outs[0], (1 - column) * half + h)
        for i in range(2):
            send(mine[2 * h + 1].at[i], outs[1 + i], column * half + h)
            send(theirs[h].at[i], outs[1 + i], (1 - column) * half + h)
    copy_all(copies)


def collected(mine, theirs, shape):
    heads = shape[0]
    return pl.pallas_call(
        functools.partial(collect_kernel, len(mine)),
        out_shape=(pltpu.HBM(shape, jnp.bfloat16),) * 3,
        in_specs=[VMEM_SPEC] * (len(mine) + len(theirs)),
        out_specs=(pl.BlockSpec(memory_space=pltpu.HBM),) * 3,
        scratch_shapes=[pltpu.SemaphoreType.DMA((3 * heads,))],
        compiler_params=SMALL_GRANT,
        name="collected",
    )(*on_chip(*mine, *theirs))


def swapped(queries, key_vectors, value_vectors, out_grad, cell_valid):
    heads, frames, tile_size, _, width = queries.shape
    tokens = frames * tile_size * tile_size
    half = heads // 2
    rows = lax.axis_size("sy")
    swap = [(0, 1), (1, 0)]
    even_pairs, odd_pairs = pairs_of(rows, 0), pairs_of(rows, 1)
    arrays = [a.reshape(heads, tokens, width) for a in (key_vectors, value_vectors, queries, out_grad)]
    later = range(1, half)

    def rows_sent(even_block, odd_block):
        return (
            lax.ppermute(even_block, "sy", even_pairs), lax.ppermute(odd_block, "sy", odd_pairs)
        )

    key_value, query_grad_pair = (0, 1), (2, 3)
    first_kv, = packed(arrays, [[(a, 0, False) for a in key_value]])
    own_kv, first_qg = packed(
        arrays,
        [[(a, h, True) for h in range(half) for a in key_value]]
        + [[(a, 0, False) for a in query_grad_pair]],
    )
    later_kv, later_qg, own_qg = packed(
        arrays,
        [[(a, h, False) for h in later for a in side] for side in (key_value, query_grad_pair)]
        + [[(a, h, True) for h in range(half) for a in query_grad_pair]],
    )
    kv_first = lax.ppermute(first_kv, "sx", swap)
    qg_first = lax.ppermute(first_qg, "sx", swap)
    kv_later = lax.ppermute(later_kv, "sx", swap)
    qg_later = lax.ppermute(later_qg, "sx", swap)
    even_own, odd_own = rows_sent(own_kv, own_kv)
    bias = window_bias(cell_valid, tile_size)
    even_first, odd_first = rows_sent(kv_first, kv_first)
    even_later, odd_later = rows_sent(kv_later, kv_later)

    own_dq, partner_dq, backs = [], [], []
    for h in range(half):
        kv, qg, even, odd = (
            (kv_later, qg_later, even_later, odd_later)
            if h
            else (kv_first, qg_first, even_first, odd_first)
        )
        sides = (own_kv, own_qg, kv, qg, even_own, even, odd_own, odd)
        grads = head_grads(h, max(2 * h - 2, 0), sides, bias)
        own_dq.append(grads[0])
        partner_dq.append(grads[1])
        backs.append((grads[2], rows_sent(grads[3], grads[4])))
    mine, theirs = [], []
    for h, (middle, (even_back, odd_back)) in enumerate(backs):
        total = middle + even_back.astype(jnp.float32) + odd_back.astype(jnp.float32)
        total = total.astype(jnp.bfloat16)
        mine += [own_dq[h], total[:2]]
        queries_out = [partner_dq[j] for j, (ref, _) in enumerate(query_slots(half)) if ref == h]
        outgoing = jnp.concatenate([total[2:]] + [q[None] for q in queries_out], axis=0)
        theirs.append(lax.ppermute(outgoing, "sx", swap))
    outs = collected(mine, theirs, (heads, tokens, width))
    return tuple(out.reshape(queries.shape) for out in outs)


def local(queries, *rest):
    if lax.axis_size("sx") == 2 and queries.shape[0] % 2 == 0 and queries.shape[0] > 2:
        return swapped(queries, *rest)
    return general(queries, *rest)


def solution(mesh):
    spec = P("tp", None, "sy", "sx", None)
    return jax.shard_map(
        local,
        mesh=mesh,
        in_specs=(spec, spec, spec, spec, P()),
        out_specs=(spec, spec, spec),
        check_vma=False,
    )
```

```python
import functools
import math

import jax
import jax.numpy as jnp
from jax import lax
from jax.experimental import pallas as pl
from jax.experimental.pallas import tpu as pltpu
from jax.sharding import PartitionSpec as P

MASKED = -1e30
VMEM_SPEC = pl.BlockSpec(memory_space=pltpu.VMEM)
SMALL_GRANT = pltpu.CompilerParams(vmem_limit_bytes=16 * 2**20)


def on_chip(*arrays):
    return [pltpu.with_memory_space_constraint(a, pltpu.VMEM) for a in arrays]


def extended(block, sides, width):
    for axis, dim in sides:
        count = lax.axis_size(axis)
        forward = [(i, i + 1) for i in range(count - 1)]
        backward = [(target, source) for source, target in forward]
        low = lax.ppermute(
            lax.slice_in_dim(block, block.shape[dim] - width, None, axis=dim), axis, forward
        )
        high = lax.ppermute(lax.slice_in_dim(block, 0, width, axis=dim), axis, backward)
        block = jnp.concatenate([low, block, high], axis=dim)
    return block


def passed_along(block, axis, distance):
    devices = range(lax.axis_size(axis))
    route = [(i - distance, i) for i in devices if i - distance in devices]
    return lax.ppermute(block, axis, route)


def window_mask(cell_rim, frames, tile_size):
    rim_span = 3 * tile_size
    offset = jnp.arange(rim_span)[None, :] - tile_size - jnp.arange(tile_size)[:, None]
    inside = jnp.abs(offset) <= tile_size
    key_ok = cell_rim == 1
    query_ok = key_ok[tile_size : 2 * tile_size, tile_size : 2 * tile_size]
    cell_pairs = (
        inside[:, None, :, None]
        & inside[None, :, None, :]
        & key_ok[None, None]
        & query_ok[:, :, None, None]
    )
    allowed = jnp.broadcast_to(
        cell_pairs[None, :, :, None], (frames, tile_size, tile_size, frames, rim_span, rim_span)
    )
    allowed = allowed.reshape(frames * tile_size * tile_size, frames * rim_span * rim_span)
    query_live = jnp.broadcast_to(query_ok[None], (frames, tile_size, tile_size)).reshape(-1)
    return (allowed, query_live)


def contract_last(left_rows, right_rows):
    return lax.dot_general(
        left_rows, right_rows, (((1,), (1,)), ((), ())), preferred_element_type=jnp.float32
    )


def contract_first(left_rows, right_rows):
    return lax.dot_general(
        left_rows, right_rows, (((0,), (0,)), ((), ())), preferred_element_type=jnp.float32
    )


def query_pass(query_rows, grad_rows, key_rows, value_rows, allowed, query_live, score_scale):
    scores = contract_last(query_rows, key_rows) * score_scale
    masked = jnp.where(allowed, scores, -jnp.inf)
    row_max = jnp.where(query_live, jnp.max(masked, axis=1), 0.0)
    unnormed = jnp.where(allowed, jnp.exp(scores - row_max[:, None]), 0.0)
    row_total = jnp.sum(unnormed, axis=1) + jnp.where(query_live, 0.0, 1.0)
    probs = unnormed / row_total[:, None]
    probs_low = probs.astype(jnp.bfloat16)
    attended = jnp.dot(probs_low, value_rows, preferred_element_type=jnp.float32)
    row_delta = jnp.sum(grad_rows.astype(jnp.float32) * attended, axis=1)
    dprobs = contract_last(grad_rows, value_rows)
    dscores_low = (probs * (dprobs - row_delta[:, None])).astype(jnp.bfloat16)
    query_part = jnp.dot(dscores_low, key_rows, preferred_element_type=jnp.float32) * score_scale
    return (probs_low, dscores_low, query_part, row_max, row_total, row_delta)


def general(queries, key_vectors, value_vectors, out_grad, cell_valid):
    tile_size = queries.shape[2]
    frames = queries.shape[1]
    width = queries.shape[-1]
    score_scale = 1.0 / math.sqrt(width)
    row_place = lax.axis_index("sy") * tile_size
    column_place = lax.axis_index("sx") * tile_size
    cell_rim = lax.dynamic_slice(
        jnp.pad(cell_valid, tile_size), (row_place, column_place), (3 * tile_size, 3 * tile_size)
    )
    allowed, query_live = window_mask(cell_rim, frames, tile_size)
    pair_local = jnp.stack([key_vectors, value_vectors], 1)
    pair_rims = extended(pair_local, (("sy", 3), ("sx", 4)), tile_size)

    def head_returned(inputs):
        query_head, grad_head, pair_rim = inputs
        query_rows = query_head.reshape(-1, width)
        grad_rows = grad_head.reshape(-1, width)
        probs_low, dscores_low, query_part, _, _, _ = query_pass(
            query_rows,
            grad_rows,
            pair_rim[0].reshape(-1, width),
            pair_rim[1].reshape(-1, width),
            allowed,
            query_live,
            score_scale,
        )
        key_part = (contract_first(dscores_low, query_rows) * score_scale).astype(jnp.bfloat16)
        value_part = contract_first(probs_low, grad_rows).astype(jnp.bfloat16)
        side_parts = jnp.stack([key_part, value_part]).reshape(pair_rim.shape)
        return (query_part.astype(jnp.bfloat16).reshape(query_head.shape), side_parts)

    query_grad, side_parts = lax.map(head_returned, (queries, out_grad, pair_rims))
    upper_band = side_parts[:, :, :, 0:tile_size]
    middle_rows = side_parts[:, :, :, tile_size : 2 * tile_size]
    lower_band = side_parts[:, :, :, 2 * tile_size : 3 * tile_size]
    below_parts = passed_along(upper_band, "sy", -1)
    above_parts = passed_along(lower_band, "sy", 1)
    row_sum = (
        middle_rows.astype(jnp.float32)
        + below_parts.astype(jnp.float32)
        + above_parts.astype(jnp.float32)
    )
    left_tile = row_sum[:, :, :, :, 0:tile_size]
    centre_tile = row_sum[:, :, :, :, tile_size : 2 * tile_size]
    right_tile = row_sum[:, :, :, :, 2 * tile_size : 3 * tile_size]
    right_parts = passed_along(left_tile, "sx", -1)
    left_parts = passed_along(right_tile, "sx", 1)
    side_total = centre_tile + right_parts + left_parts
    key_grad = side_total[:, 0].astype(jnp.bfloat16)
    value_grad = side_total[:, 1].astype(jnp.bfloat16)
    return (query_grad, key_grad, value_grad)


def pairs_of(count, first, groups):
    route = []
    for group in range(groups):
        for row in range(count):
            other = row + 1 if (row - first) % 2 == 0 else row - 1
            if 0 <= other < count:
                route.append((group * count + row, group * count + other))
            elif groups % 2 == 0:
                route.append((group * count + row, (group ^ 1) * count + row))
    return route


def neighbour_rows(row):
    return row + 1 - 2 * lax.rem(row, 2), row - 1 + 2 * lax.rem(row, 2)


def copy_all(copies):
    for copy in copies:
        copy.start()
    for copy in copies:
        copy.wait()


def pack_kernel(picks, *refs):
    arrays, outs, sems = refs[:4], refs[4:-1], refs[-1]
    half = arrays[0].shape[0] // 2
    column = lax.axis_index("sx")
    copies = []
    for out, rows in zip(outs, picks):
        for slot, (array, h, mine) in enumerate(rows):
            head = (column if mine else 1 - column) * half + h
            copies.append(
                pltpu.make_async_copy(
                    arrays[array].at[head], out.at[slot], sems.at[len(copies)]
                )
            )
    copy_all(copies)


def packed(arrays, picks):
    tokens, width = arrays[0].shape[1:]
    return pl.pallas_call(
        functools.partial(pack_kernel, picks),
        out_shape=tuple(pltpu.VMEM((len(rows), tokens, width), jnp.bfloat16) for rows in picks),
        in_specs=[pl.BlockSpec(memory_space=pltpu.HBM)] * 4,
        out_specs=tuple(VMEM_SPEC for _ in picks),
        scratch_shapes=[pltpu.SemaphoreType.DMA((sum(map(len, picks)),))],
        compiler_params=SMALL_GRANT,
    )(*[pltpu.with_memory_space_constraint(a, pltpu.HBM) for a in arrays])


def bias_kernel(tile_size, valid_ref, bias_ref):
    row, column = lax.axis_index("sy"), lax.axis_index("sx")
    tile_rows = (row, *neighbour_rows(row))
    tile_columns = (column, 1 - column)
    valid = valid_ref[...] == 1
    rows = lax.broadcasted_iota(jnp.int32, valid.shape, 0)
    columns = lax.broadcasted_iota(jnp.int32, valid.shape, 1)
    far = max(valid.shape)
    top = jnp.min(jnp.where(valid, rows, far))
    bottom = jnp.max(jnp.where(valid, rows, -1))
    left = jnp.min(jnp.where(valid, columns, far))
    right = jnp.max(jnp.where(valid, columns, -1))
    shape = bias_ref.shape[2:]
    key_cell = lax.broadcasted_iota(jnp.int32, shape, 0)
    query_cell = lax.broadcasted_iota(jnp.int32, shape, 1) % (tile_size * tile_size)
    key_row, key_column = key_cell // tile_size, key_cell % tile_size
    query_row, query_column = query_cell // tile_size, query_cell % tile_size

    def inside(r, c):
        return (r >= top) & (r <= bottom) & (c >= left) & (c <= right)

    for b in range(2):
        q_row = query_row + row * tile_size
        q_column = query_column + tile_columns[b] * tile_size
        q_ok = inside(q_row, q_column)
        for t in range(6):
            k_row = key_row + tile_rows[t // 2] * tile_size
            k_column = key_column + tile_columns[t % 2] * tile_size
            near = (jnp.abs(k_row - q_row) <= tile_size) & (
                jnp.abs(k_column - q_column) <= tile_size
            )
            ok = near & q_ok & inside(k_row, k_column)
            bias_ref[b, t] = jnp.where(ok, 0.0, MASKED)


def window_bias(cell_valid, tile_size):
    cells = tile_size * tile_size
    return pl.pallas_call(
        functools.partial(bias_kernel, tile_size),
        out_shape=pltpu.VMEM((2, 6, cells, 2 * cells), jnp.float32),
        in_specs=[VMEM_SPEC],
        out_specs=VMEM_SPEC,
        compiler_params=SMALL_GRANT,
        name="window_bias",
    )(cell_valid)


def head_kernel(
    h, place,
    own_kv_ref, own_qg_ref, kv_ref, qg_ref, even_own_ref, even_ref, odd_own_ref, odd_ref, bias_ref,
    own_dq_ref, partner_dq_ref, middle_ref, even_part_ref, odd_part_ref,
    score_ref, dprob_ref, key_sum_ref, value_sum_ref,
):
    tokens, width = own_kv_ref.shape[1:]
    score_scale = 1.0 / math.sqrt(width)
    exponent_scale = math.log2(math.e) / math.sqrt(width)
    sides = ((own_kv_ref, kv_ref), (even_own_ref, even_ref), (odd_own_ref, odd_ref))
    keys, values = [
        [ref.at[first + i] for side in sides for ref, first in zip(side, (2 * h, place))]
        for i in range(2)
    ]
    key_parts, value_parts = [
        [part.at[2 * c + i] for part in (middle_ref, even_part_ref, odd_part_ref) for c in range(2)]
        for i in range(2)
    ]
    blocks = (
        (own_qg_ref[2 * h], own_qg_ref[2 * h + 1], own_dq_ref),
        (qg_ref[place], qg_ref[place + 1], partner_dq_ref),
    )
    for b, (query_rows, grad_rows, dq_ref) in enumerate(blocks):
        row_max = None
        for t in range(6):
            bias = bias_ref[b, t]
            bias = jnp.concatenate([bias] * (tokens // bias.shape[1]), axis=1)
            bias = jnp.concatenate([bias] * (tokens // bias.shape[0]), axis=0)
            scores = contract_last(keys[t][...], query_rows) + bias
            score_ref[t] = scores
            tile_max = jnp.max(scores, axis=0, keepdims=True)
            row_max = tile_max if row_max is None else jnp.maximum(row_max, tile_max)
        live = row_max > 0.5 * MASKED
        row_max = jnp.where(live, row_max, 0.0)
        row_total = jnp.where(live, 0.0, 1.0)
        row_delta = jnp.zeros_like(row_max)
        for t in range(6):
            unnormed = jnp.exp2((score_ref[t] - row_max) * exponent_scale)
            dprobs = contract_last(values[t][...], grad_rows)
            score_ref[t] = unnormed
            dprob_ref[t] = dprobs
            row_total = row_total + jnp.sum(unnormed, axis=0, keepdims=True)
            row_delta = row_delta + jnp.sum(unnormed * dprobs, axis=0, keepdims=True)
        inverse = 1.0 / row_total
        row_delta = row_delta * inverse
        query_grad = None
        for t in range(6):
            probs = score_ref[t] * inverse
            dscores_low = (probs * (dprob_ref[t] - row_delta)).astype(jnp.bfloat16)
            value_part = jnp.dot(
                probs.astype(jnp.bfloat16), grad_rows, preferred_element_type=jnp.float32
            )
            key_part = jnp.dot(dscores_low, query_rows, preferred_element_type=jnp.float32)
            if b == 0:
                key_sum_ref[t] = key_part
                value_sum_ref[t] = value_part
            else:
                key_total = (key_sum_ref[t] + key_part) * score_scale
                key_parts[t][...] = key_total.astype(key_parts[t].dtype)
                value_total = value_sum_ref[t] + value_part
                value_parts[t][...] = value_total.astype(value_parts[t].dtype)
            query_part = contract_first(dscores_low, keys[t][...])
            query_grad = query_part if query_grad is None else query_grad + query_part
        dq_ref[...] = (query_grad * score_scale).astype(jnp.bfloat16)


def head_grads(h, place, arrays, bias):
    tokens, width = arrays[0].shape[1:]
    low = jnp.bfloat16
    pairs = 2 * 6 * tokens * tokens
    return pl.pallas_call(
        functools.partial(head_kernel, h, place),
        out_shape=(
            pltpu.VMEM((tokens, width), low),
            pltpu.VMEM((tokens, width), low),
            pltpu.VMEM((4, tokens, width), jnp.float32),
            pltpu.VMEM((4, tokens, width), low),
            pltpu.VMEM((4, tokens, width), low),
        ),
        in_specs=[VMEM_SPEC] * 9,
        out_specs=[VMEM_SPEC] * 5,
        scratch_shapes=[
            pltpu.VMEM((6, tokens, tokens), jnp.float32),
            pltpu.VMEM((6, tokens, tokens), jnp.float32),
            pltpu.VMEM((6, tokens, width), jnp.float32),
            pltpu.VMEM((6, tokens, width), jnp.float32),
        ],
        compiler_params=SMALL_GRANT,
        cost_estimate=pl.CostEstimate(
            flops=10 * pairs * width, transcendentals=pairs, bytes_accessed=20 * tokens * width * 2
        ),
        name="head_grads",
    )(*on_chip(*arrays, bias))


def query_slots(half):
    return [(0, 2)] + [(h - 1, 2 + (h == 1)) for h in range(1, half)]


def collect_kernel(count, *refs):
    mine, theirs, outs, sems = refs[:count], refs[count:-4], refs[-4:-1], refs[-1]
    half = outs[0].shape[0] // 2
    column = lax.axis_index("sx")
    copies = []

    def send(source, out, head):
        copies.append(pltpu.make_async_copy(source, out.at[head], sems.at[len(copies)]))

    for h, (ref, slot) in enumerate(query_slots(half)):
        send(mine[2 * h], outs[0], column * half + h)
        send(theirs[ref].at[slot], outs[0], (1 - column) * half + h)
        for i in range(2):
            send(mine[2 * h + 1].at[i], outs[1 + i], column * half + h)
            send(theirs[h].at[i], outs[1 + i], (1 - column) * half + h)
    copy_all(copies)


def collected(mine, theirs, shape):
    heads = shape[0]
    return pl.pallas_call(
        functools.partial(collect_kernel, len(mine)),
        out_shape=(pltpu.HBM(shape, jnp.bfloat16),) * 3,
        in_specs=[VMEM_SPEC] * (len(mine) + len(theirs)),
        out_specs=(pl.BlockSpec(memory_space=pltpu.HBM),) * 3,
        scratch_shapes=[pltpu.SemaphoreType.DMA((3 * heads,))],
        compiler_params=SMALL_GRANT,
        name="collected",
    )(*on_chip(*mine, *theirs))


def swapped(queries, key_vectors, value_vectors, out_grad, cell_valid):
    heads, frames, tile_size, _, width = queries.shape
    tokens = frames * tile_size * tile_size
    half = heads // 2
    rows = lax.axis_size("sy")
    swap = [(0, 1), (1, 0)]
    even_pairs, odd_pairs = [pairs_of(rows, first, lax.axis_size("tp")) for first in range(2)]
    arrays = [a.reshape(heads, tokens, width) for a in (key_vectors, value_vectors, queries, out_grad)]
    later = range(1, half)

    def rows_sent(even_block, odd_block):
        return (
            lax.ppermute(even_block, ("tp", "sy"), even_pairs),
            lax.ppermute(odd_block, ("tp", "sy"), odd_pairs),
        )

    key_value, query_grad_pair = (0, 1), (2, 3)
    first_kv, = packed(arrays, [[(a, 0, False) for a in key_value]])
    own_kv, first_qg = packed(
        arrays,
        [[(a, h, True) for h in range(half) for a in key_value]]
        + [[(a, 0, False) for a in query_grad_pair]],
    )
    later_kv, later_qg, own_qg = packed(
        arrays,
        [[(a, h, False) for h in later for a in side] for side in (key_value, query_grad_pair)]
        + [[(a, h, True) for h in range(half) for a in query_grad_pair]],
    )
    kv_first = lax.ppermute(first_kv, "sx", swap)
    qg_first = lax.ppermute(first_qg, "sx", swap)
    kv_later = lax.ppermute(later_kv, "sx", swap)
    qg_later = lax.ppermute(later_qg, "sx", swap)
    even_own, odd_own = rows_sent(own_kv, own_kv)
    bias = window_bias(cell_valid, tile_size)
    even_first, odd_first = rows_sent(kv_first, kv_first)
    even_later, odd_later = rows_sent(kv_later, kv_later)

    own_dq, partner_dq, backs = [], [], []
    for h in range(half):
        kv, qg, even, odd = (
            (kv_later, qg_later, even_later, odd_later)
            if h
            else (kv_first, qg_first, even_first, odd_first)
        )
        sides = (own_kv, own_qg, kv, qg, even_own, even, odd_own, odd)
        grads = head_grads(h, max(2 * h - 2, 0), sides, bias)
        own_dq.append(grads[0])
        partner_dq.append(grads[1])
        backs.append((grads[2], rows_sent(grads[3], grads[4])))
    mine, theirs = [], []
    for h, (middle, (even_back, odd_back)) in enumerate(backs):
        total = middle + even_back.astype(jnp.float32) + odd_back.astype(jnp.float32)
        total = total.astype(jnp.bfloat16)
        mine += [own_dq[h], total[:2]]
        queries_out = [partner_dq[j] for j, (ref, _) in enumerate(query_slots(half)) if ref == h]
        outgoing = jnp.concatenate([total[2:]] + [q[None] for q in queries_out], axis=0)
        theirs.append(lax.ppermute(outgoing, "sx", swap))
    outs = collected(mine, theirs, (heads, tokens, width))
    return tuple(out.reshape(queries.shape) for out in outs)


def local(queries, *rest):
    if lax.axis_size("sx") == 2 and queries.shape[0] % 2 == 0 and queries.shape[0] > 2:
        return swapped(queries, *rest)
    return general(queries, *rest)


def solution(mesh):
    spec = P("tp", None, "sy", "sx", None)
    return jax.shard_map(
        local,
        mesh=mesh,
        in_specs=(spec, spec, spec, spec, P()),
        out_specs=(spec, spec, spec),
        check_vma=False,
    )
```

```python
import functools
import math

import jax
import jax.numpy as jnp
from jax import lax
from jax.experimental import pallas as pl
from jax.experimental.pallas import tpu as pltpu
from jax.sharding import PartitionSpec as P

MASKED = -1e30
VMEM_SPEC = pl.BlockSpec(memory_space=pltpu.VMEM)
SMALL_GRANT = pltpu.CompilerParams(vmem_limit_bytes=16 * 2**20)


def on_chip(*arrays):
    return [pltpu.with_memory_space_constraint(a, pltpu.VMEM) for a in arrays]


def extended(block, sides, width):
    for axis, dim in sides:
        count = lax.axis_size(axis)
        forward = [(i, i + 1) for i in range(count - 1)]
        backward = [(target, source) for source, target in forward]
        low = lax.ppermute(
            lax.slice_in_dim(block, block.shape[dim] - width, None, axis=dim), axis, forward
        )
        high = lax.ppermute(lax.slice_in_dim(block, 0, width, axis=dim), axis, backward)
        block = jnp.concatenate([low, block, high], axis=dim)
    return block


def passed_along(block, axis, distance):
    devices = range(lax.axis_size(axis))
    route = [(i - distance, i) for i in devices if i - distance in devices]
    return lax.ppermute(block, axis, route)


def window_mask(cell_rim, frames, tile_size):
    rim_span = 3 * tile_size
    offset = jnp.arange(rim_span)[None, :] - tile_size - jnp.arange(tile_size)[:, None]
    inside = jnp.abs(offset) <= tile_size
    key_ok = cell_rim == 1
    query_ok = key_ok[tile_size : 2 * tile_size, tile_size : 2 * tile_size]
    cell_pairs = (
        inside[:, None, :, None]
        & inside[None, :, None, :]
        & key_ok[None, None]
        & query_ok[:, :, None, None]
    )
    allowed = jnp.broadcast_to(
        cell_pairs[None, :, :, None], (frames, tile_size, tile_size, frames, rim_span, rim_span)
    )
    allowed = allowed.reshape(frames * tile_size * tile_size, frames * rim_span * rim_span)
    query_live = jnp.broadcast_to(query_ok[None], (frames, tile_size, tile_size)).reshape(-1)
    return (allowed, query_live)


def contract_last(left_rows, right_rows):
    return lax.dot_general(
        left_rows, right_rows, (((1,), (1,)), ((), ())), preferred_element_type=jnp.float32
    )


def contract_first(left_rows, right_rows):
    return lax.dot_general(
        left_rows, right_rows, (((0,), (0,)), ((), ())), preferred_element_type=jnp.float32
    )


def query_pass(query_rows, grad_rows, key_rows, value_rows, allowed, query_live, score_scale):
    scores = contract_last(query_rows, key_rows) * score_scale
    masked = jnp.where(allowed, scores, -jnp.inf)
    row_max = jnp.where(query_live, jnp.max(masked, axis=1), 0.0)
    unnormed = jnp.where(allowed, jnp.exp(scores - row_max[:, None]), 0.0)
    row_total = jnp.sum(unnormed, axis=1) + jnp.where(query_live, 0.0, 1.0)
    probs = unnormed / row_total[:, None]
    probs_low = probs.astype(jnp.bfloat16)
    attended = jnp.dot(probs_low, value_rows, preferred_element_type=jnp.float32)
    row_delta = jnp.sum(grad_rows.astype(jnp.float32) * attended, axis=1)
    dprobs = contract_last(grad_rows, value_rows)
    dscores_low = (probs * (dprobs - row_delta[:, None])).astype(jnp.bfloat16)
    query_part = jnp.dot(dscores_low, key_rows, preferred_element_type=jnp.float32) * score_scale
    return (probs_low, dscores_low, query_part, row_max, row_total, row_delta)


def general(queries, key_vectors, value_vectors, out_grad, cell_valid):
    tile_size = queries.shape[2]
    frames = queries.shape[1]
    width = queries.shape[-1]
    score_scale = 1.0 / math.sqrt(width)
    row_place = lax.axis_index("sy") * tile_size
    column_place = lax.axis_index("sx") * tile_size
    cell_rim = lax.dynamic_slice(
        jnp.pad(cell_valid, tile_size), (row_place, column_place), (3 * tile_size, 3 * tile_size)
    )
    allowed, query_live = window_mask(cell_rim, frames, tile_size)
    pair_local = jnp.stack([key_vectors, value_vectors], 1)
    pair_rims = extended(pair_local, (("sy", 3), ("sx", 4)), tile_size)

    def head_returned(inputs):
        query_head, grad_head, pair_rim = inputs
        query_rows = query_head.reshape(-1, width)
        grad_rows = grad_head.reshape(-1, width)
        probs_low, dscores_low, query_part, _, _, _ = query_pass(
            query_rows,
            grad_rows,
            pair_rim[0].reshape(-1, width),
            pair_rim[1].reshape(-1, width),
            allowed,
            query_live,
            score_scale,
        )
        key_part = (contract_first(dscores_low, query_rows) * score_scale).astype(jnp.bfloat16)
        value_part = contract_first(probs_low, grad_rows).astype(jnp.bfloat16)
        side_parts = jnp.stack([key_part, value_part]).reshape(pair_rim.shape)
        return (query_part.astype(jnp.bfloat16).reshape(query_head.shape), side_parts)

    query_grad, side_parts = lax.map(head_returned, (queries, out_grad, pair_rims))
    upper_band = side_parts[:, :, :, 0:tile_size]
    middle_rows = side_parts[:, :, :, tile_size : 2 * tile_size]
    lower_band = side_parts[:, :, :, 2 * tile_size : 3 * tile_size]
    below_parts = passed_along(upper_band, "sy", -1)
    above_parts = passed_along(lower_band, "sy", 1)
    row_sum = (
        middle_rows.astype(jnp.float32)
        + below_parts.astype(jnp.float32)
        + above_parts.astype(jnp.float32)
    )
    left_tile = row_sum[:, :, :, :, 0:tile_size]
    centre_tile = row_sum[:, :, :, :, tile_size : 2 * tile_size]
    right_tile = row_sum[:, :, :, :, 2 * tile_size : 3 * tile_size]
    right_parts = passed_along(left_tile, "sx", -1)
    left_parts = passed_along(right_tile, "sx", 1)
    side_total = centre_tile + right_parts + left_parts
    key_grad = side_total[:, 0].astype(jnp.bfloat16)
    value_grad = side_total[:, 1].astype(jnp.bfloat16)
    return (query_grad, key_grad, value_grad)


def pairs_of(count, first, groups):
    route = []
    for group in range(groups):
        for row in range(count):
            other = row + 1 if (row - first) % 2 == 0 else row - 1
            if 0 <= other < count:
                route.append((group * count + row, group * count + other))
            elif groups % 2 == 0:
                route.append((group * count + row, (group ^ 1) * count + row))
    return route


def neighbour_rows(row):
    return row + 1 - 2 * lax.rem(row, 2), row - 1 + 2 * lax.rem(row, 2)


def copy_all(copies):
    for copy in copies:
        copy.start()
    for copy in copies:
        copy.wait()


def pack_kernel(picks, *refs):
    arrays, outs, sems = refs[:4], refs[4:-1], refs[-1]
    half = arrays[0].shape[0] // 2
    column = lax.axis_index("sx")
    copies = []
    for out, rows in zip(outs, picks):
        for slot, (array, h, mine) in enumerate(rows):
            head = (column if mine else 1 - column) * half + h
            copies.append(
                pltpu.make_async_copy(
                    arrays[array].at[head], out.at[slot], sems.at[len(copies)]
                )
            )
    copy_all(copies)


def packed(arrays, picks):
    tokens, width = arrays[0].shape[1:]
    return pl.pallas_call(
        functools.partial(pack_kernel, picks),
        out_shape=tuple(pltpu.VMEM((len(rows), tokens, width), jnp.bfloat16) for rows in picks),
        in_specs=[pl.BlockSpec(memory_space=pltpu.HBM)] * 4,
        out_specs=tuple(VMEM_SPEC for _ in picks),
        scratch_shapes=[pltpu.SemaphoreType.DMA((sum(map(len, picks)),))],
        compiler_params=SMALL_GRANT,
    )(*[pltpu.with_memory_space_constraint(a, pltpu.HBM) for a in arrays])


def bias_kernel(tile_size, valid_ref, bias_ref):
    row, column = lax.axis_index("sy"), lax.axis_index("sx")
    tile_rows = (row, *neighbour_rows(row))
    tile_columns = (column, 1 - column)
    valid = valid_ref[...] == 1
    rows = lax.broadcasted_iota(jnp.int32, valid.shape, 0)
    columns = lax.broadcasted_iota(jnp.int32, valid.shape, 1)
    far = max(valid.shape)
    top = jnp.min(jnp.where(valid, rows, far))
    bottom = jnp.max(jnp.where(valid, rows, -1))
    left = jnp.min(jnp.where(valid, columns, far))
    right = jnp.max(jnp.where(valid, columns, -1))
    shape = bias_ref.shape[2:]
    key_cell = lax.broadcasted_iota(jnp.int32, shape, 0)
    query_cell = lax.broadcasted_iota(jnp.int32, shape, 1) % (tile_size * tile_size)
    key_row, key_column = key_cell // tile_size, key_cell % tile_size
    query_row, query_column = query_cell // tile_size, query_cell % tile_size

    def inside(r, c):
        return (r >= top) & (r <= bottom) & (c >= left) & (c <= right)

    for b in range(2):
        q_row = query_row + row * tile_size
        q_column = query_column + tile_columns[b] * tile_size
        q_ok = inside(q_row, q_column)
        for t in range(6):
            k_row = key_row + tile_rows[t // 2] * tile_size
            k_column = key_column + tile_columns[t % 2] * tile_size
            near = (jnp.abs(k_row - q_row) <= tile_size) & (
                jnp.abs(k_column - q_column) <= tile_size
            )
            ok = near & q_ok & inside(k_row, k_column)
            bias_ref[b, t] = jnp.where(ok, 0.0, MASKED)


def window_bias(cell_valid, tile_size):
    cells = tile_size * tile_size
    return pl.pallas_call(
        functools.partial(bias_kernel, tile_size),
        out_shape=pltpu.VMEM((2, 6, cells, 2 * cells), jnp.float32),
        in_specs=[VMEM_SPEC],
        out_specs=VMEM_SPEC,
        compiler_params=SMALL_GRANT,
        name="window_bias",
    )(cell_valid)


def head_kernel(
    h,
    own_kv_ref, own_qg_ref, kv_ref, qg_ref, even_own_ref, even_ref, odd_own_ref, odd_ref, bias_ref,
    own_dq_ref, partner_dq_ref, middle_ref, even_part_ref, odd_part_ref,
    score_ref, dprob_ref, key_sum_ref, value_sum_ref,
):
    tokens, width = own_kv_ref.shape[1:]
    score_scale = 1.0 / math.sqrt(width)
    exponent_scale = math.log2(math.e) / math.sqrt(width)
    sides = ((own_kv_ref, kv_ref), (even_own_ref, even_ref), (odd_own_ref, odd_ref))
    keys, values = [
        [ref.at[first + i] for side in sides for ref, first in zip(side, (2 * h, 0))]
        for i in range(2)
    ]
    key_parts, value_parts = [
        [part.at[2 * c + i] for part in (middle_ref, even_part_ref, odd_part_ref) for c in range(2)]
        for i in range(2)
    ]
    blocks = (
        (own_qg_ref[2 * h], own_qg_ref[2 * h + 1], own_dq_ref),
        (qg_ref[0], qg_ref[1], partner_dq_ref),
    )
    for b, (query_rows, grad_rows, dq_ref) in enumerate(blocks):
        row_max = None
        for t in range(6):
            bias = bias_ref[b, t]
            bias = jnp.concatenate([bias] * (tokens // bias.shape[1]), axis=1)
            bias = jnp.concatenate([bias] * (tokens // bias.shape[0]), axis=0)
            scores = contract_last(keys[t][...], query_rows) + bias
            score_ref[t] = scores
            tile_max = jnp.max(scores, axis=0, keepdims=True)
            row_max = tile_max if row_max is None else jnp.maximum(row_max, tile_max)
        live = row_max > 0.5 * MASKED
        row_max = jnp.where(live, row_max, 0.0)
        row_total = jnp.where(live, 0.0, 1.0)
        row_delta = jnp.zeros_like(row_max)
        for t in range(6):
            unnormed = jnp.exp2((score_ref[t] - row_max) * exponent_scale)
            dprobs = contract_last(values[t][...], grad_rows)
            score_ref[t] = unnormed
            dprob_ref[t] = dprobs
            row_total = row_total + jnp.sum(unnormed, axis=0, keepdims=True)
            row_delta = row_delta + jnp.sum(unnormed * dprobs, axis=0, keepdims=True)
        inverse = 1.0 / row_total
        row_delta = row_delta * inverse
        query_grad = None
        for t in range(6):
            probs = score_ref[t] * inverse
            dscores_low = (probs * (dprob_ref[t] - row_delta)).astype(jnp.bfloat16)
            value_part = jnp.dot(
                probs.astype(jnp.bfloat16), grad_rows, preferred_element_type=jnp.float32
            )
            key_part = jnp.dot(dscores_low, query_rows, preferred_element_type=jnp.float32)
            if b == 0:
                key_sum_ref[t] = key_part
                value_sum_ref[t] = value_part
            else:
                key_total = (key_sum_ref[t] + key_part) * score_scale
                key_parts[t][...] = key_total.astype(key_parts[t].dtype)
                value_total = value_sum_ref[t] + value_part
                value_parts[t][...] = value_total.astype(value_parts[t].dtype)
            query_part = contract_first(dscores_low, keys[t][...])
            query_grad = query_part if query_grad is None else query_grad + query_part
        dq_ref[...] = (query_grad * score_scale).astype(jnp.bfloat16)


def head_grads(h, arrays, bias):
    tokens, width = arrays[0].shape[1:]
    low = jnp.bfloat16
    pairs = 2 * 6 * tokens * tokens
    return pl.pallas_call(
        functools.partial(head_kernel, h),
        out_shape=(
            pltpu.VMEM((tokens, width), low),
            pltpu.VMEM((tokens, width), low),
            pltpu.VMEM((4, tokens, width), jnp.float32),
            pltpu.VMEM((4, tokens, width), low),
            pltpu.VMEM((4, tokens, width), low),
        ),
        in_specs=[VMEM_SPEC] * 9,
        out_specs=[VMEM_SPEC] * 5,
        scratch_shapes=[
            pltpu.VMEM((6, tokens, tokens), jnp.float32),
            pltpu.VMEM((6, tokens, tokens), jnp.float32),
            pltpu.VMEM((6, tokens, width), jnp.float32),
            pltpu.VMEM((6, tokens, width), jnp.float32),
        ],
        compiler_params=SMALL_GRANT,
        cost_estimate=pl.CostEstimate(
            flops=10 * pairs * width, transcendentals=pairs, bytes_accessed=20 * tokens * width * 2
        ),
        name="head_grads",
    )(*on_chip(*arrays, bias))


def query_slots(half):
    return [(0, 2)] + [(h - 1, 2 + (h == 1)) for h in range(1, half)]


def collect_kernel(count, *refs):
    mine, theirs, outs, sems = refs[:count], refs[count:-4], refs[-4:-1], refs[-1]
    half = outs[0].shape[0] // 2
    column = lax.axis_index("sx")
    copies = []

    def send(source, out, head):
        copies.append(pltpu.make_async_copy(source, out.at[head], sems.at[len(copies)]))

    for h, (ref, slot) in enumerate(query_slots(half)):
        send(mine[2 * h], outs[0], column * half + h)
        send(theirs[ref].at[slot], outs[0], (1 - column) * half + h)
        for i in range(2):
            send(mine[2 * h + 1].at[i], outs[1 + i], column * half + h)
            send(theirs[h].at[i], outs[1 + i], (1 - column) * half + h)
    copy_all(copies)


def collected(mine, theirs, shape):
    heads = shape[0]
    return pl.pallas_call(
        functools.partial(collect_kernel, len(mine)),
        out_shape=(pltpu.HBM(shape, jnp.bfloat16),) * 3,
        in_specs=[VMEM_SPEC] * (len(mine) + len(theirs)),
        out_specs=(pl.BlockSpec(memory_space=pltpu.HBM),) * 3,
        scratch_shapes=[pltpu.SemaphoreType.DMA((3 * heads,))],
        compiler_params=SMALL_GRANT,
        name="collected",
    )(*on_chip(*mine, *theirs))


def swapped(queries, key_vectors, value_vectors, out_grad, cell_valid):
    heads, frames, tile_size, _, width = queries.shape
    tokens = frames * tile_size * tile_size
    half = heads // 2
    rows = lax.axis_size("sy")
    swap = [(0, 1), (1, 0)]
    even_pairs, odd_pairs = [pairs_of(rows, first, lax.axis_size("tp")) for first in range(2)]
    arrays = [a.reshape(heads, tokens, width) for a in (key_vectors, value_vectors, queries, out_grad)]
    later = range(1, half)

    def rows_sent(even_block, odd_block):
        return (
            lax.ppermute(even_block, ("tp", "sy"), even_pairs),
            lax.ppermute(odd_block, ("tp", "sy"), odd_pairs),
        )

    key_value, query_and_grad = (0, 1), (2, 3)

    def picks(head_range, side, mine):
        return [(a, h, mine) for h in head_range for a in side]

    kv_out, qg_out = [None] * half, [None] * half
    kv_out[0], = packed(arrays, [picks([0], key_value, False)])
    own_kv, qg_out[0] = packed(
        arrays, [picks(range(half), key_value, True), picks([0], query_and_grad, False)]
    )
    own_qg, *rest = packed(
        arrays,
        [picks(range(half), query_and_grad, True)]
        + [picks([h], side, False) for side in (key_value, query_and_grad) for h in later],
    )
    kv_out[1:], qg_out[1:] = rest[: half - 1], rest[half - 1 :]
    kv = [lax.ppermute(kv_out[h], "sx", swap) for h in range(half)]
    qg = [lax.ppermute(qg_out[h], "sx", swap) for h in range(half)]
    even_own, odd_own = rows_sent(own_kv, own_kv)
    bias = window_bias(cell_valid, tile_size)

    own_dq, partner_dq, backs = [], [], []
    for h in range(half):
        even, odd = rows_sent(kv[h], kv[h])
        grads = head_grads(h, (own_kv, own_qg, kv[h], qg[h], even_own, even, odd_own, odd), bias)
        own_dq.append(grads[0])
        partner_dq.append(grads[1])
        backs.append((grads[2], rows_sent(grads[3], grads[4])))
    mine, theirs = [], []
    for h, (middle, (even_back, odd_back)) in enumerate(backs):
        total = middle + even_back.astype(jnp.float32) + odd_back.astype(jnp.float32)
        total = total.astype(jnp.bfloat16)
        mine += [own_dq[h], total[:2]]
        queries_out = [partner_dq[j] for j, (ref, _) in enumerate(query_slots(half)) if ref == h]
        outgoing = jnp.concatenate([total[2:]] + [q[None] for q in queries_out], axis=0)
        theirs.append(lax.ppermute(outgoing, "sx", swap))
    outs = collected(mine, theirs, (heads, tokens, width))
    return tuple(out.reshape(queries.shape) for out in outs)


def swaps_heads(mesh, queries):
    half, rest = divmod(queries.shape[0], 2 * mesh.shape["tp"])
    return mesh.shape["sx"] == 2 and rest == 0 and half > 1


def solution(mesh):
    spec = P("tp", None, "sy", "sx", None)

    def mapped(body):
        return jax.shard_map(
            body,
            mesh=mesh,
            in_specs=(spec, spec, spec, spec, P()),
            out_specs=(spec, spec, spec),
            check_vma=False,
        )

    def step(queries, key_vectors, value_vectors, out_grad, cell_valid):
        arrays = (queries, key_vectors, value_vectors, out_grad, cell_valid)
        if not swaps_heads(mesh, queries):
            return mapped(general)(*arrays)
        return mapped(swapped)(*arrays)

    return step
```
